32 devices in a mesh: narrow: 4 (over y, x), region: 8 (over z, core).
Axes of the slice: x: 2, y: 2, z: 4, core: 2. Of those that a mesh axis runs over, the one named last changes fastest.
Arguments:
- point_feats: bfloat16 [64, 131072], P(None, ('narrow', 'region')), may hold values from -6 to 6
- point_owner: int32 [131072, 1], P(('narrow', 'region')), may hold values from 0 to 31; in each aligned block of 4096 rows (0 to 4095, 4096 to 8191, ...) at most 256 rows name the same one
- point_voxel: int32 [131072], P(('narrow', 'region')), may hold values from 0 to 12287
- weight: bfloat16 [9, 64, 192], replicated, may hold values from -0.15625 to 0.15625
- cotangent: bfloat16 [64, 192, 2048], P(None, 'region', 'narrow'), may hold values from -6 to 6
Outputs:
- conv_out: bfloat16 [64, 192, 2048], P(None, 'region', 'narrow')
- point_grad: bfloat16 [64, 131072], P(None, ('narrow', 'region'))
- weight_grad: float32 [9, 64, 192], replicated
The draws below stay inside these ranges and needn't reach their ends.
Inputs may be any that keep to these rules, and one draw needn't show every extreme that they name: `point_owner`: among the 4096 points of one device no owner is named more than 256 times, a bound that some block reaches.
All inputs are finite; a program needn't handle non-finite values.
Results may differ from the reference program's by a relative error of at most 0.0036.
Values may be sent and summed in bfloat16 or wider, within the bound.
A program may use at most 192 MiB of HBM per device.

```python
import math
import jax
import jax.numpy as jnp
import numpy as np
from jax import lax

C = 64
NZ = 64
CY = 8
CX = 24
P_DEV = 4096
CAP = 256
VOX_DEV = 12288
NX = 192
NY = 32
POINTS = 131072
N_REGION = 8
DEVICES = 32


def with_ends(drawn, own_key, least, top_value):
    index_at = [jax.random.randint(jax.random.fold_in(own_key, axis), (), 0, length) for axis, length in enumerate(drawn.shape)]
    main_axis = drawn.shape.index(max(drawn.shape))
    beside = index_at[:main_axis] + [(index_at[main_axis] + 1) % drawn.shape[main_axis]] + index_at[main_axis + 1:]
    return drawn.at[tuple(index_at)].set(least).at[tuple(beside)].set(top_value)


def levels(rng, dims, split, low, largest):
    gain, own = 1.0, jax.random.fold_in(rng, 6)
    for position, shards_of in split:
        heights = jnp.exp(jax.random.uniform(jax.random.fold_in(own, position), (shards_of,), jnp.float32, low / len(split), largest / len(split)))
        gain = gain * jnp.repeat(heights, dims[position] // shards_of).reshape([-1 if axis == position else 1 for axis in range(len(dims))])
    return gain


def deal_out(key, own, number, rows, count, top, bound, slope):
    order = jax.random.permutation(key, count)
    heavy_load, usual = load_shares(count, rows * top, bound, slope, True), load_shares(count, rows * top, bound, slope, False)
    places = jnp.arange(count)

    def named(tallies, offset_by):
        used = int((tallies > 0).sum())
        fixed = max(1, used // 4)
        passed = fixed + (places - fixed + offset_by * (used - fixed)) % max(1, count - fixed)
        return jnp.zeros((count,), jnp.int32).at[order[jnp.where(places < fixed, places, passed)]].set(jnp.asarray(tallies, jnp.int32))

    tallies = jnp.where(number % 4 == 0, named(heavy_load, number // 4), named(usual, number - number // 4 - 1))
    mixed = jax.random.permutation(jax.random.fold_in(own, 3), count)
    giver, sink = mixed[0:count // 2 * 2:2], mixed[1:count // 2 * 2:2]
    slack = jnp.minimum(tallies[giver] - 1, bound - tallies[sink]) // 2
    slack = jnp.where((giver == order[0]) | (sink == order[0]) | (tallies[sink] == 0), 0, jnp.maximum(slack, 0))
    passed = jax.random.randint(jax.random.fold_in(own, 4), (count // 2,), 0, 1 << 20) % (slack + 1)
    tallies = tallies.at[giver].add(-passed).at[sink].add(passed)
    members = jnp.searchsorted(jnp.cumsum(tallies), jnp.arange(rows * top), side="right").astype(jnp.int32)
    listing = members.reshape(top, rows).T
    listing = listing[jax.random.permutation(jax.random.fold_in(own, 1), rows)]
    offset_by = jax.random.randint(jax.random.fold_in(own, 2), (rows, 1), 0, top)
    return jnp.take_along_axis(listing, (jnp.arange(top)[None, :] + offset_by) % top, axis=1)


def load_shares(amount, total, bound, skew, full):
    portions = [(1 << 20) // math.isqrt(grade ** skew) + 1 for grade in range(1, amount + 1)]
    largest = bound if full else min(bound, max(-(-total // amount), total * portions[0] // sum(portions)))
    least = 1 if total - largest >= amount - 1 else 0
    holding, surplus = [largest] + [least] * (amount - 1), total - largest - least * (amount - 1)
    while surplus > 0:
        movable = [i for i in range(1, amount) if holding[i] < largest] or [i for i in range(1, amount) if holding[i] < bound]
        pool, budget = sum([portions[i] for i in movable]), surplus
        for i in movable:
            addition = min(bound - holding[i], max(1, budget * portions[i] // pool), surplus)
            holding[i] = holding[i] + addition
            surplus = surplus - addition
    return np.array(holding)


def bell_draw(stream_key, dims, deviation, bound, pieces=(), held_as=jnp.bfloat16):
    values = jax.random.normal(stream_key, dims, jnp.float32) * deviation
    if len(pieces) > 0:
        values = levels(stream_key, dims, pieces, -0.22, 0.18) * values
    return jnp.clip(values, min=-bound, max=bound).astype(held_as)


def setup_inputs(seed: int = 0) -> dict:
    keys = jax.random.split(jax.random.key(seed), 6)
    point_feats = bell_draw(keys[0], (C, POINTS), 1.0, 6.0, ((1, 32),))
    point_owner_keys = jax.random.split(jax.random.fold_in(keys[1], 1), POINTS // P_DEV)
    point_owner_turns = jax.random.permutation(jax.random.fold_in(keys[1], 3), POINTS // P_DEV)
    point_owner = jax.vmap(lambda own, number: deal_out(jax.random.fold_in(keys[1], 2), own, number, P_DEV, DEVICES, 1, CAP, 2))(point_owner_keys, point_owner_turns).reshape((POINTS, 1))
    point_voxel = with_ends(jax.random.randint(keys[2], (POINTS,), 0, VOX_DEV), jax.random.fold_in(keys[2], 1), 0, VOX_DEV - 1).astype(jnp.int32)
    weight = bell_draw(keys[3], (9, C, 3 * C), (27 * C) ** -0.5, 0.15625)
    cotangent = bell_draw(keys[4], (C, NX, NY * NZ), 1.0, 6.0, ((1, 8), (2, 4)))
    return dict(point_feats=point_feats, point_owner=point_owner, point_voxel=point_voxel, weight=weight, cotangent=cotangent)


def stack_depth(padded, offsets, depth):
    return jnp.concatenate([padded[..., o:o + depth] for o in offsets], axis=0)

def reference(point_feats, point_owner, point_voxel, weight, cotangent):
    owner = point_owner[:, 0]
    narrow_idx = owner // N_REGION
    region_idx = owner % N_REGION
    local_x = point_voxel // (CY * NZ)
    local_y = point_voxel // NZ % CY
    local_z = point_voxel % NZ
    flat = (((region_idx * CX + local_x) * NY + narrow_idx * CY + local_y) * NZ + local_z).astype(jnp.int32)
    sums = jax.ops.segment_sum(point_feats.astype(jnp.float32).T, flat, num_segments=NX * NY * NZ)
    grid = sums.T.astype(jnp.bfloat16).reshape(C, NX, NY, NZ)
    padded = jnp.pad(grid, ((0, 0), (1, 1), (1, 1), (1, 1)))
    stacked = stack_depth(padded, [0, 1, 2], NZ)
    grads = cotangent.reshape(C, NX, NY, NZ)
    gpad = jnp.pad(grads, ((0, 0), (1, 1), (1, 1), (1, 1)))
    gstack = stack_depth(gpad, [2, 1, 0], NZ)
    flipped = weight.reshape(9, C, 3, C).transpose(0, 3, 2, 1).reshape(9, C, 3 * C)

    def slab(index):
        start = (index * CX).astype(jnp.int32)
        xs = lax.dynamic_slice_in_dim(stacked, start, CX + 2, 1).astype(jnp.float32)
        gs = lax.dynamic_slice_in_dim(gstack, start, CX + 2, 1).astype(jnp.float32)
        gl = lax.dynamic_slice_in_dim(grads, start, CX, 1).astype(jnp.float32)
        result = jnp.zeros((C, CX, NY, NZ), jnp.float32)
        backward = jnp.zeros((C, CX, NY, NZ), jnp.float32)
        kernels = []
        for a in range(3):
            for b in range(3):
                k = a * 3 + b
                window = xs[:, a:a + CX, b:b + NY]
                result = result + jnp.einsum('ok,kxyz->oxyz', weight[k].astype(jnp.float32), window)
                kernels.append(jnp.einsum('oxyz,kxyz->ok', gl, window))
                backward = backward + jnp.einsum('ck,kxyz->cxyz', flipped[k].astype(jnp.float32), gs[:, 2 - a:2 - a + CX, 2 - b:2 - b + NY])
        return (result, backward, jnp.stack(kernels))
    results, backwards, kernels = lax.map(slab, jnp.arange(N_REGION, dtype=jnp.int32))
    conv_out = results.transpose(1, 0, 2, 3, 4).reshape(C, NX, NY * NZ).astype(jnp.bfloat16)
    grad_grid = backwards.transpose(1, 0, 2, 3, 4).reshape(C, NX * NY * NZ).astype(jnp.bfloat16)
    point_grad = jnp.take(grad_grid, flat, axis=1)
    weight_grad = lax.optimization_barrier(jnp.sum(kernels, axis=0)) * (1.0 / math.sqrt(NX * NY * NZ))
    return (conv_out, point_grad, weight_grad)
```

```python
import functools
import math

import jax
import jax.numpy as jnp
from jax import lax
from jax.experimental import pallas as pl
from jax.experimental.pallas import tpu as pltpu
from jax.sharding import PartitionSpec as P

NZ = 64
CY = 8
AXES = ("narrow", "region")
GROUP = 8
TILE = 512


def extended(cells, sides):
    for axis, dim in sides:
        count = lax.axis_size(axis)
        ends = count - 1
        head = lax.slice_in_dim(cells, 0, 1, axis=dim)
        tail = lax.slice_in_dim(cells, cells.shape[dim] - 1, cells.shape[dim], axis=dim)
        cells = jnp.concatenate(
            [
                lax.ppermute(tail, axis, [(i, (i + 1) % count) for i in range(ends)]),
                cells,
                lax.ppermute(head, axis, [((i + 1) % count, i) for i in range(ends)]),
            ],
            axis=dim,
        )
    return cells


def stacked_depth(cells):
    padded = extended(cells, (("narrow", 1), ("region", 0)))
    padded = jnp.pad(padded, ((0, 0), (0, 0), (1, 1), (0, 0)))
    return jnp.concatenate([padded[:, :, d : d + NZ] for d in range(3)], axis=3)


def convolved(stack, kernel):
    return lax.conv_general_dilated(
        stack,
        kernel,
        (1, 1),
        "VALID",
        dimension_numbers=lax.ConvDimensionNumbers((2, 3, 0, 1), (3, 2, 0, 1), (2, 3, 0, 1)),
        preferred_element_type=jnp.float32,
    )


def packed(buf, out_ref):
    rows = out_ref.shape[0]

    def tile(t, _):
        low = pl.multiple_of(t * TILE, TILE)
        left = buf[pl.ds(low, TILE), :]
        right = buf[pl.ds(rows + low, TILE), :]
        out_ref[pl.ds(low, TILE), :] = jnp.concatenate([left, right], axis=1).astype(jnp.bfloat16)

    lax.fori_loop(0, rows // TILE, tile, None)


def unpacked(in_ref, buf):
    rows, lanes = in_ref.shape

    def tile(t, _):
        low = pl.multiple_of(t * TILE, TILE)
        both = in_ref[pl.ds(low, TILE), :].astype(jnp.float32)
        buf[pl.ds(low, TILE), :] = both[:, : lanes // 2]
        buf[pl.ds(rows + low, TILE), :] = both[:, lanes // 2 :]

    lax.fori_loop(0, rows // TILE, tile, None)


def each_arrival(devices, slots, rows, count_ref, visit):
    half = slots // 2

    def source(s, _):
        here = count_ref[s]
        for h in range(2):
            some = jnp.clip(here - h * half, 0, half)

            def group(j, _):
                for u in range(GROUP):
                    r = j * GROUP + u
                    visit(u, s * slots + h * half + r, h * rows + s * half + r)

            lax.fori_loop(0, (some + GROUP - 1) // GROUP, group, None)

    lax.fori_loop(0, devices, source, None)


def place_kernel(place_ref, vox_ref, rows_ref, out_ref, vox_out_ref, buf):
    def group(j, _):
        for u in range(GROUP):
            p = j * GROUP + u
            d = place_ref[p]
            buf[pl.ds(d, 1), :] = rows_ref[pl.ds(p, 1), :]
            vox_out_ref[d] = vox_ref[p]

    lax.fori_loop(0, rows_ref.shape[0] // GROUP, group, None)
    packed(buf, out_ref)


def splat_kernel(devices, slots, vox_ref, count_ref, got_ref, grid_ref, buf, *sums):
    unpacked(got_ref, buf)
    voxels, chans = grid_ref.shape

    def clear(t, _):
        for each in sums:
            each[pl.ds(pl.multiple_of(t * TILE, TILE), TILE), :] = jnp.zeros((TILE, chans), jnp.float32)

    lax.fori_loop(0, voxels // TILE, clear, None)

    def visit(u, k, r):
        v = vox_ref[k]
        each = sums[u % len(sums)]
        each[pl.ds(v, 1), :] += buf[pl.ds(r, 1), :]

    each_arrival(devices, slots, got_ref.shape[0], count_ref, visit)

    def finish(t, _):
        at = pl.ds(pl.multiple_of(t * TILE, TILE), TILE)
        total = sums[0][at, :]
        for each in sums[1:]:
            total += each[at, :]
        grid_ref[at, :] = total.astype(jnp.bfloat16)

    lax.fori_loop(0, voxels // TILE, finish, None)


def pick_kernel(devices, slots, vox_ref, count_ref, table_ref, out_ref, buf):
    def visit(u, k, r):
        buf[pl.ds(r, 1), :] = table_ref[pl.ds(vox_ref[k], 1), :]

    each_arrival(devices, slots, out_ref.shape[0], count_ref, visit)
    packed(buf, out_ref)


def collect_kernel(place_ref, back_ref, out_ref, buf):
    unpacked(back_ref, buf)

    def group(j, _):
        for u in range(GROUP):
            p = j * GROUP + u
            out_ref[pl.ds(p, 1), :] = buf[pl.ds(place_ref[p], 1), :]

    lax.fori_loop(0, out_ref.shape[0] // GROUP, group, None)


def call(kernel, out_shape, kinds, out_kinds, scratch, cost, *operands):
    where = {"s": pltpu.SMEM, "v": pltpu.VMEM}
    specs = [pl.BlockSpec(memory_space=where[k]) for k in out_kinds]
    return pl.pallas_call(
        kernel,
        out_shape=out_shape,
        in_specs=[pl.BlockSpec(memory_space=where[k]) for k in kinds],
        out_specs=specs if len(specs) > 1 else specs[0],
        scratch_shapes=scratch,
        compiler_params=pltpu.CompilerParams(vmem_limit_bytes=50 << 20),
        cost_estimate=pl.CostEstimate(flops=0, bytes_accessed=cost, transcendentals=0),
    )(*operands)


def ranks(owner, devices):
    span = 128
    chunks = owner.shape[0] // span
    marks = owner.reshape(chunks, span)[:, :, None] == jnp.arange(devices, dtype=jnp.int32)
    ones = marks.astype(jnp.bfloat16)
    before = (jnp.arange(span)[:, None] > jnp.arange(span)[None, :]).astype(jnp.bfloat16)
    inner = jnp.einsum("ij,cjo->cio", before, ones, preferred_element_type=jnp.float32)
    tallies = jnp.sum(ones.astype(jnp.float32), axis=1)
    ahead = (jnp.arange(chunks)[:, None] > jnp.arange(chunks)[None, :]).astype(jnp.bfloat16)
    starts = jnp.einsum("ij,jo->io", ahead, tallies.astype(jnp.bfloat16), preferred_element_type=jnp.float32)
    slot = jnp.sum(jnp.where(marks, inner + starts[:, None, :], 0.0), axis=2)
    return slot.reshape(-1).astype(jnp.int32), jnp.sum(tallies, axis=0).astype(jnp.int32)


def exchanged(x):
    return lax.all_to_all(x, AXES, split_axis=0, concat_axis=0, tiled=True)


def shards(point_feats, point_owner, point_voxel, weight, cotangent):
    n_narrow = lax.axis_size("narrow")
    n_region = lax.axis_size("region")
    devices = n_narrow * n_region
    chans, points_here = point_feats.shape
    slots = 2 * points_here // devices
    half = slots // 2
    rows = devices * half
    rows_x = cotangent.shape[1]
    voxels = rows_x * CY * NZ
    f32, bf16, i32 = jnp.float32, jnp.bfloat16, jnp.int32
    buffer = pltpu.VMEM((2 * rows, chans), f32)
    pairs = jax.ShapeDtypeStruct((rows, 2 * chans), bf16)

    owner = point_owner[:, 0]
    slot, sent = ranks(owner, devices)
    place = (slot // half) * rows + owner * half + slot % half
    send, send_vox = call(
        place_kernel,
        (pairs, jax.ShapeDtypeStruct((2 * rows,), i32)),
        "ssv",
        "vs",
        [buffer],
        40 << 20,
        place,
        point_voxel,
        point_feats.T.astype(f32),
    )
    send_vox = send_vox.reshape(2, devices, half).transpose(1, 0, 2).reshape(devices, slots)
    filled = jnp.arange(slots, dtype=i32)[None, :] < sent[:, None]
    got_vox = exchanged(jnp.where(filled, send_vox, voxels))
    got = exchanged(send.reshape(devices, half, 2 * chans)).reshape(rows, 2 * chans)
    count = jnp.sum((got_vox < voxels).astype(i32), axis=1)
    add_at = got_vox.reshape(-1)
    pick_at = jnp.where(got_vox < voxels, got_vox, 0).reshape(-1)

    w = weight.reshape(3, 3, chans, 3, chans)
    backward = w[::-1, ::-1, :, ::-1, :].transpose(0, 1, 3, 2, 4).reshape(3, 3, 3 * chans, chans)
    forward = weight.reshape(3, 3, chans, 3 * chans).transpose(0, 1, 3, 2)

    grads = cotangent.reshape(chans, rows_x, CY, NZ).transpose(1, 2, 3, 0)
    table = convolved(stacked_depth(grads), backward).reshape(voxels, chans)
    picked = call(
        functools.partial(pick_kernel, devices, slots),
        pairs,
        "ssv",
        "v",
        [buffer],
        40 << 20,
        pick_at,
        count,
        table,
    )
    back = exchanged(picked.reshape(devices, half, 2 * chans)).reshape(rows, 2 * chans)

    grid = call(
        functools.partial(splat_kernel, devices, slots),
        jax.ShapeDtypeStruct((voxels, chans), bf16),
        "ssv",
        "v",
        [buffer] + [pltpu.VMEM((voxels + 8, chans), f32)] * 4,
        80 << 20,
        add_at,
        count,
        got,
    )
    stack = stacked_depth(grid.reshape(rows_x, CY, NZ, chans))
    flat = cotangent.reshape(chans, voxels)
    kernels = []
    for a in range(3):
        for b in range(3):
            window = stack[a : a + rows_x, b : b + CY].reshape(voxels, 3 * chans)
            kernels.append(jnp.einsum("ov,vk->ok", flat, window, preferred_element_type=f32))
    total_cells = rows_x * n_region * CY * n_narrow * NZ
    parts = exchanged(jnp.stack(kernels).reshape(devices, -1))
    mine = jnp.sum(parts, axis=0) * (1.0 / math.sqrt(total_cells))
    weight_grad = lax.all_gather(mine, AXES, tiled=True).reshape(9, chans, 3 * chans)

    result = convolved(stack, forward).astype(bf16)
    conv_out = result.transpose(3, 0, 1, 2).reshape(chans, rows_x, CY * NZ)

    point_rows = call(
        collect_kernel,
        jax.ShapeDtypeStruct((points_here, chans), f32),
        "sv",
        "v",
        [buffer],
        40 << 20,
        place,
        back,
    )
    return (conv_out, point_rows.T.astype(bf16), weight_grad)


def solution(mesh):
    in_specs = (
        P(None, AXES),
        P(AXES, None),
        P(AXES),
        P(),
        P(None, "region", "narrow"),
    )
    out_specs = (P(None, "region", "narrow"), P(None, AXES), P())
    return jax.shard_map(shards, mesh=mesh, in_specs=in_specs, out_specs=out_specs, check_vma=False)
```

```python
import functools
import math

import jax
import jax.numpy as jnp
from jax import lax
from jax.experimental import pallas as pl
from jax.experimental.pallas import tpu as pltpu
from jax.sharding import PartitionSpec as P

NZ = 64
CY = 8
AXES = ("narrow", "region")
GROUP = 8
TILE = 512


def halo_kernel(n_narrow, n_region, grid, left, right, top, bottom, send, recv):
    n, r = lax.axis_index("narrow"), lax.axis_index("region")
    west, east = lax.rem(n + n_narrow - 1, n_narrow), lax.rem(n + 1, n_narrow)
    north, south = lax.rem(r + n_region - 1, n_region), lax.rem(r + 1, n_region)
    last = grid.shape[0] - 1
    moves = [
        ((west, r), grid.at[:, 0], right),
        ((east, r), grid.at[:, CY - 1], left),
        ((n, north), grid.at[0], bottom.at[pl.ds(1, CY)]),
        ((n, south), grid.at[last], top.at[pl.ds(1, CY)]),
        ((west, north), grid.at[0, 0], bottom.at[CY + 1]),
        ((east, north), grid.at[0, CY - 1], bottom.at[0]),
        ((west, south), grid.at[last, 0], top.at[CY + 1]),
        ((east, south), grid.at[last, CY - 1], top.at[0]),
    ]
    barrier = pltpu.get_barrier_semaphore()
    for device, _, _ in moves:
        pl.semaphore_signal(barrier, inc=1, device_id=device, device_id_type=pl.DeviceIdType.MESH)
    pl.semaphore_wait(barrier, len(moves))
    copies = [
        pltpu.make_async_remote_copy(
            src_ref=source,
            dst_ref=target,
            send_sem=send.at[i],
            recv_sem=recv.at[i],
            device_id=device,
            device_id_type=pl.DeviceIdType.MESH,
        )
        for i, (device, source, target) in enumerate(moves)
    ]
    for copy in copies:
        copy.start()
    for copy in copies:
        copy.wait()


def halos(grid, n_narrow, n_region, collective_id):
    rows_x, _, depth, chans = grid.shape
    side = jax.ShapeDtypeStruct((rows_x, depth, chans), grid.dtype)
    end = jax.ShapeDtypeStruct((CY + 2, depth, chans), grid.dtype)
    anywhere = pl.BlockSpec(memory_space=pl.ANY)
    return pl.pallas_call(
        functools.partial(halo_kernel, n_narrow, n_region),
        out_shape=(side, side, end, end),
        in_specs=[anywhere],
        out_specs=[anywhere] * 4,
        scratch_shapes=[pltpu.SemaphoreType.DMA((8,)), pltpu.SemaphoreType.DMA((8,))],
        compiler_params=pltpu.CompilerParams(collective_id=collective_id, has_side_effects=True),
        cost_estimate=pl.CostEstimate(flops=0, bytes_accessed=10 << 20, transcendentals=0),
    )(grid)


def stack_kernel(inside_ref, center, left, right, top, bottom, out):
    rows_x, _, depth, chans = center.shape
    f32 = jnp.float32
    row = lax.broadcasted_iota(jnp.int32, (depth, chans), 0)
    west, east, north, south = [inside_ref[i] for i in range(4)]

    def spread(tile, keep=None):
        t = tile.astype(f32)
        if keep is not None:
            t = jnp.where(keep > 0, t, 0.0)
        up = jnp.where(row == 0, 0.0, pltpu.roll(t, 1, 0))
        down = jnp.where(row == depth - 1, 0.0, pltpu.roll(t, depth - 1, 0))
        return jnp.concatenate([up, t, down], axis=1).astype(jnp.bfloat16)

    def plane(x, _):
        out[x + 1, 0] = spread(left[x], west)
        out[x + 1, CY + 1] = spread(right[x], east)
        for y in range(CY):
            out[x + 1, y + 1] = spread(center[x, y])

    lax.fori_loop(0, rows_x, plane, None)
    for at, end, keep in ((0, top, north), (rows_x + 1, bottom, south)):
        out[at, 0] = spread(end[0], keep * west)
        out[at, CY + 1] = spread(end[CY + 1], keep * east)
        for y in range(1, CY + 1):
            out[at, y] = spread(end[y], keep)


def stack_weight_kernel(inside_ref, center, left, right, top, bottom, flat, out, sums):
    stack_kernel(inside_ref, center, left, right, top, bottom, out)
    sums[...] = jnp.zeros_like(sums)
    plane_cells = CY * NZ

    def plane(x, _):
        here = flat[:, pl.ds(pl.multiple_of(x * plane_cells, plane_cells), plane_cells)]
        for a in range(3):
            for b in range(3):
                window = out[x + a, b : b + CY].reshape(plane_cells, out.shape[3])
                sums[3 * a + b] += jnp.dot(here, window, preferred_element_type=jnp.float32)

    lax.fori_loop(0, center.shape[0], plane, None)


def stacked_depth(cells, n_narrow, n_region, collective_id, flat=None):
    rows_x, _, depth, chans = cells.shape
    n, r = lax.axis_index("narrow"), lax.axis_index("region")
    inside = jnp.stack([n > 0, n < n_narrow - 1, r > 0, r < n_region - 1]).astype(jnp.int32)
    edges = halos(cells, n_narrow, n_region, collective_id)
    stack = jax.ShapeDtypeStruct((rows_x + 2, CY + 2, depth, 3 * chans), cells.dtype)
    if flat is None:
        return call(stack_kernel, stack, "svvvvv", "v", [], 40 << 20, inside, cells, *edges)
    sums = jax.ShapeDtypeStruct((9, chans, 3 * chans), jnp.float32)
    return call(
        stack_weight_kernel, (stack, sums), "svvvvvv", "vv", [], 80 << 20, inside, cells, *edges, flat
    )


def convolved(stack, kernel):
    return lax.conv_general_dilated(
        stack,
        kernel,
        (1, 1),
        "VALID",
        dimension_numbers=lax.ConvDimensionNumbers((2, 3, 0, 1), (3, 2, 0, 1), (2, 3, 0, 1)),
        preferred_element_type=jnp.float32,
    )


def packed(buf, out_ref):
    rows = out_ref.shape[0]

    def tile(t, _):
        low = pl.multiple_of(t * TILE, TILE)
        left = buf[pl.ds(low, TILE), :]
        right = buf[pl.ds(rows + low, TILE), :]
        out_ref[pl.ds(low, TILE), :] = jnp.concatenate([left, right], axis=1).astype(jnp.bfloat16)

    lax.fori_loop(0, rows // TILE, tile, None)


def unpacked(in_ref, buf):
    rows, lanes = in_ref.shape

    def tile(t, _):
        low = pl.multiple_of(t * TILE, TILE)
        both = in_ref[pl.ds(low, TILE), :].astype(jnp.float32)
        buf[pl.ds(low, TILE), :] = both[:, : lanes // 2]
        buf[pl.ds(rows + low, TILE), :] = both[:, lanes // 2 :]

    lax.fori_loop(0, rows // TILE, tile, None)


def each_arrival(devices, slots, rows, count_ref, visit):
    half = slots // 2

    def source(s, _):
        here = count_ref[s]
        for h in range(2):
            some = jnp.clip(here - h * half, 0, half)

            def group(j, _):
                for u in range(GROUP):
                    r = j * GROUP + u
                    visit(u, s * slots + h * half + r, h * rows + s * half + r)

            lax.fori_loop(0, (some + GROUP - 1) // GROUP, group, None)

    lax.fori_loop(0, devices, source, None)


def place_kernel(place_ref, vox_ref, rows_ref, out_ref, vox_out_ref, buf):
    def group(j, _):
        for u in range(GROUP):
            p = j * GROUP + u
            d = place_ref[p]
            buf[pl.ds(d, 1), :] = rows_ref[pl.ds(p, 1), :]
            vox_out_ref[d] = vox_ref[p]

    lax.fori_loop(0, rows_ref.shape[0] // GROUP, group, None)
    packed(buf, out_ref)


def splat_kernel(devices, slots, vox_ref, count_ref, got_ref, grid_ref, buf, *sums):
    unpacked(got_ref, buf)
    voxels, chans = grid_ref.shape

    def clear(t, _):
        for each in sums:
            each[pl.ds(pl.multiple_of(t * TILE, TILE), TILE), :] = jnp.zeros((TILE, chans), jnp.float32)

    lax.fori_loop(0, voxels // TILE, clear, None)

    def visit(u, k, r):
        v = vox_ref[k]
        each = sums[u % len(sums)]
        each[pl.ds(v, 1), :] += buf[pl.ds(r, 1), :]

    each_arrival(devices, slots, got_ref.shape[0], count_ref, visit)

    def finish(t, _):
        at = pl.ds(pl.multiple_of(t * TILE, TILE), TILE)
        total = sums[0][at, :]
        for each in sums[1:]:
            total += each[at, :]
        grid_ref[at, :] = total.astype(jnp.bfloat16)

    lax.fori_loop(0, voxels // TILE, finish, None)


def pick_kernel(devices, slots, vox_ref, count_ref, table_ref, out_ref, buf):
    def visit(u, k, r):
        buf[pl.ds(r, 1), :] = table_ref[pl.ds(vox_ref[k], 1), :]

    each_arrival(devices, slots, out_ref.shape[0], count_ref, visit)
    packed(buf, out_ref)


def collect_kernel(place_ref, back_ref, out_ref, buf):
    unpacked(back_ref, buf)

    def group(j, _):
        for u in range(GROUP):
            p = j * GROUP + u
            out_ref[pl.ds(p, 1), :] = buf[pl.ds(place_ref[p], 1), :]

    lax.fori_loop(0, out_ref.shape[0] // GROUP, group, None)


def call(kernel, out_shape, kinds, out_kinds, scratch, cost, *operands):
    where = {"s": pltpu.SMEM, "v": pltpu.VMEM}
    specs = [pl.BlockSpec(memory_space=where[k]) for k in out_kinds]
    return pl.pallas_call(
        kernel,
        out_shape=out_shape,
        in_specs=[pl.BlockSpec(memory_space=where[k]) for k in kinds],
        out_specs=specs if len(specs) > 1 else specs[0],
        scratch_shapes=scratch,
        compiler_params=pltpu.CompilerParams(vmem_limit_bytes=50 << 20),
        cost_estimate=pl.CostEstimate(flops=0, bytes_accessed=cost, transcendentals=0),
    )(*operands)


def ranks(owner, devices):
    span = 128
    chunks = owner.shape[0] // span
    marks = owner.reshape(chunks, span)[:, :, None] == jnp.arange(devices, dtype=jnp.int32)
    ones = marks.astype(jnp.bfloat16)
    before = (jnp.arange(span)[:, None] > jnp.arange(span)[None, :]).astype(jnp.bfloat16)
    inner = jnp.einsum("ij,cjo->cio", before, ones, preferred_element_type=jnp.float32)
    tallies = jnp.sum(ones.astype(jnp.float32), axis=1)
    ahead = (jnp.arange(chunks)[:, None] > jnp.arange(chunks)[None, :]).astype(jnp.bfloat16)
    starts = jnp.einsum("ij,jo->io", ahead, tallies.astype(jnp.bfloat16), preferred_element_type=jnp.float32)
    slot = jnp.sum(jnp.where(marks, inner + starts[:, None, :], 0.0), axis=2)
    return slot.reshape(-1).astype(jnp.int32), jnp.sum(tallies, axis=0).astype(jnp.int32)


def exchanged(x):
    return lax.all_to_all(x, AXES, split_axis=0, concat_axis=0, tiled=True)


def shards(point_feats, point_owner, point_voxel, weight, cotangent):
    n_narrow = lax.axis_size("narrow")
    n_region = lax.axis_size("region")
    devices = n_narrow * n_region
    chans, points_here = point_feats.shape
    slots = 2 * points_here // devices
    half = slots // 2
    rows = devices * half
    rows_x = cotangent.shape[1]
    voxels = rows_x * CY * NZ
    f32, bf16, i32 = jnp.float32, jnp.bfloat16, jnp.int32
    buffer = pltpu.VMEM((2 * rows, chans), f32)
    pairs = jax.ShapeDtypeStruct((rows, 2 * chans), bf16)

    owner = point_owner[:, 0]
    slot, sent = ranks(owner, devices)
    place = (slot // half) * rows + owner * half + slot % half
    send, send_vox = call(
        place_kernel,
        (pairs, jax.ShapeDtypeStruct((2 * rows,), i32)),
        "ssv",
        "vs",
        [buffer],
        40 << 20,
        place,
        point_voxel,
        point_feats.T.astype(f32),
    )
    send_vox = send_vox.reshape(2, devices, half).transpose(1, 0, 2).reshape(devices, slots)
    filled = jnp.arange(slots, dtype=i32)[None, :] < sent[:, None]
    got_vox = exchanged(jnp.where(filled, send_vox, voxels))
    got = exchanged(send.reshape(devices, half, 2 * chans)).reshape(rows, 2 * chans)
    count = jnp.sum((got_vox < voxels).astype(i32), axis=1)
    add_at = got_vox.reshape(-1)
    pick_at = jnp.where(got_vox < voxels, got_vox, 0).reshape(-1)

    w = weight.reshape(3, 3, chans, 3, chans)
    backward = w[::-1, ::-1, :, ::-1, :].transpose(0, 1, 3, 2, 4).reshape(3, 3, 3 * chans, chans)
    forward = weight.reshape(3, 3, chans, 3 * chans).transpose(0, 1, 3, 2)

    grads = cotangent.reshape(chans, rows_x, CY, NZ).transpose(1, 2, 3, 0)
    table = convolved(stacked_depth(grads, n_narrow, n_region, 0), backward).reshape(voxels, chans)
    picked = call(
        functools.partial(pick_kernel, devices, slots),
        pairs,
        "ssv",
        "v",
        [buffer],
        40 << 20,
        pick_at,
        count,
        table,
    )
    back = exchanged(picked.reshape(devices, half, 2 * chans)).reshape(rows, 2 * chans)

    grid = call(
        functools.partial(splat_kernel, devices, slots),
        jax.ShapeDtypeStruct((voxels, chans), bf16),
        "ssv",
        "v",
        [buffer] + [pltpu.VMEM((voxels + 8, chans), f32)] * 4,
        80 << 20,
        add_at,
        count,
        got,
    )
    cells = grid.reshape(rows_x, CY, NZ, chans)
    stack, kernels = stacked_depth(cells, n_narrow, n_region, 1, cotangent.reshape(chans, voxels))
    total_cells = rows_x * n_region * CY * n_narrow * NZ
    parts = exchanged(kernels.reshape(devices, -1))
    mine = jnp.sum(parts, axis=0) * (1.0 / math.sqrt(total_cells))
    back, mine = lax.optimization_barrier((back, mine))
    everywhere = exchanged(jnp.broadcast_to(mine, (devices, mine.shape[0])))
    weight_grad = everywhere.reshape(9, chans, 3 * chans)

    result = convolved(stack, forward).astype(bf16)
    conv_out = result.transpose(3, 0, 1, 2).reshape(chans, rows_x, CY * NZ)

    point_rows = call(
        collect_kernel,
        jax.ShapeDtypeStruct((points_here, chans), f32),
        "sv",
        "v",
        [buffer],
        40 << 20,
        place,
        back,
    )
    return (conv_out, point_rows.T.astype(bf16), weight_grad)


def solution(mesh):
    in_specs = (
        P(None, AXES),
        P(AXES, None),
        P(AXES),
        P(),
        P(None, "region", "narrow"),
    )
    out_specs = (P(None, "region", "narrow"), P(None, AXES), P())
    return jax.shard_map(shards, mesh=mesh, in_specs=in_specs, out_specs=out_specs, check_vma=False)
```

```python
import functools
import math

import jax
import jax.numpy as jnp
from jax import lax
from jax.experimental import pallas as pl
from jax.experimental.pallas import tpu as pltpu
from jax.sharding import PartitionSpec as P

NZ = 64
CY = 8
AXES = ("narrow", "region")
GROUP = 8
TILE = 512


def halo_kernel(n_narrow, n_region, grid, left, right, top, bottom, send, recv):
    n, r = lax.axis_index("narrow"), lax.axis_index("region")
    west, east = lax.rem(n + n_narrow - 1, n_narrow), lax.rem(n + 1, n_narrow)
    north, south = lax.rem(r + n_region - 1, n_region), lax.rem(r + 1, n_region)
    last = grid.shape[0] - 1
    moves = [
        ((west, r), grid.at[:, 0], right),
        ((east, r), grid.at[:, CY - 1], left),
        ((n, north), grid.at[0], bottom.at[pl.ds(1, CY)]),
        ((n, south), grid.at[last], top.at[pl.ds(1, CY)]),
        ((west, north), grid.at[0, 0], bottom.at[CY + 1]),
        ((east, north), grid.at[0, CY - 1], bottom.at[0]),
        ((west, south), grid.at[last, 0], top.at[CY + 1]),
        ((east, south), grid.at[last, CY - 1], top.at[0]),
    ]
    barrier = pltpu.get_barrier_semaphore()
    for device, _, _ in moves:
        pl.semaphore_signal(barrier, inc=1, device_id=device, device_id_type=pl.DeviceIdType.MESH)
    pl.semaphore_wait(barrier, len(moves))
    copies = [
        pltpu.make_async_remote_copy(
            src_ref=source,
            dst_ref=target,
            send_sem=send.at[i],
            recv_sem=recv.at[i],
            device_id=device,
            device_id_type=pl.DeviceIdType.MESH,
        )
        for i, (device, source, target) in enumerate(moves)
    ]
    for copy in copies:
        copy.start()
    for copy in copies:
        copy.wait()


def halos(grid, n_narrow, n_region, collective_id):
    rows_x, _, depth, chans = grid.shape
    side = jax.ShapeDtypeStruct((rows_x, depth, chans), grid.dtype)
    end = jax.ShapeDtypeStruct((CY + 2, depth, chans), grid.dtype)
    anywhere = pl.BlockSpec(memory_space=pl.ANY)
    return pl.pallas_call(
        functools.partial(halo_kernel, n_narrow, n_region),
        out_shape=(side, side, end, end),
        in_specs=[anywhere],
        out_specs=[anywhere] * 4,
        scratch_shapes=[pltpu.SemaphoreType.DMA((8,)), pltpu.SemaphoreType.DMA((8,))],
        compiler_params=pltpu.CompilerParams(collective_id=collective_id, has_side_effects=True),
        cost_estimate=pl.CostEstimate(flops=0, bytes_accessed=10 << 20, transcendentals=0),
    )(grid)


def stack_kernel(inside_ref, center, *refs):
    far, (out, left, right, top, bottom, arrived) = refs[:4], refs[-6:]
    copies = [
        pltpu.make_async_copy(source, target, arrived.at[i])
        for i, (source, target) in enumerate(zip(far, (left, right, top, bottom)))
    ]
    for copy in copies:
        copy.start()
    rows_x, _, depth, chans = center.shape
    f32 = jnp.float32
    row = lax.broadcasted_iota(jnp.int32, (depth, chans), 0)
    west, east, north, south = [inside_ref[i] for i in range(4)]

    def spread(tile, keep=None):
        t = tile.astype(f32)
        if keep is not None:
            t = jnp.where(keep > 0, t, 0.0)
        up = jnp.where(row == 0, 0.0, pltpu.roll(t, 1, 0))
        down = jnp.where(row == depth - 1, 0.0, pltpu.roll(t, depth - 1, 0))
        return jnp.concatenate([up, t, down], axis=1).astype(jnp.bfloat16)

    def plane(x, _):
        for y in range(CY):
            out[x + 1, y + 1] = spread(center[x, y])

    def sides(x, _):
        out[x + 1, 0] = spread(left[x], west)
        out[x + 1, CY + 1] = spread(right[x], east)

    lax.fori_loop(0, rows_x, plane, None)
    for copy in copies:
        copy.wait()
    lax.fori_loop(0, rows_x, sides, None)
    for at, end, keep in ((0, top, north), (rows_x + 1, bottom, south)):
        out[at, 0] = spread(end[0], keep * west)
        out[at, CY + 1] = spread(end[CY + 1], keep * east)
        for y in range(1, CY + 1):
            out[at, y] = spread(end[y], keep)


def stack_weight_kernel(inside_ref, center, left, right, top, bottom, flat, out, sums, *scratch):
    stack_kernel(inside_ref, center, left, right, top, bottom, out, *scratch)
    sums[...] = jnp.zeros_like(sums)
    plane_cells = CY * NZ

    def plane(x, _):
        here = flat[:, pl.ds(pl.multiple_of(x * plane_cells, plane_cells), plane_cells)]
        for a in range(3):
            for b in range(3):
                window = out[x + a, b : b + CY].reshape(plane_cells, out.shape[3])
                sums[3 * a + b] += jnp.dot(here, window, preferred_element_type=jnp.float32)

    lax.fori_loop(0, center.shape[0], plane, None)


def stacked_depth(cells, edges, n_narrow, n_region, flat=None):
    rows_x, _, depth, chans = cells.shape
    n, r = lax.axis_index("narrow"), lax.axis_index("region")
    inside = jnp.stack([n > 0, n < n_narrow - 1, r > 0, r < n_region - 1]).astype(jnp.int32)
    stack = jax.ShapeDtypeStruct((rows_x + 2, CY + 2, depth, 3 * chans), cells.dtype)
    scratch = [pltpu.VMEM(e.shape, e.dtype) for e in edges] + [pltpu.SemaphoreType.DMA((4,))]
    if flat is None:
        return call(stack_kernel, stack, "svaaaa", "v", scratch, 40 << 20, inside, cells, *edges)
    sums = jax.ShapeDtypeStruct((9, chans, 3 * chans), jnp.float32)
    return call(
        stack_weight_kernel,
        (stack, sums),
        "svaaaav",
        "vv",
        scratch,
        80 << 20,
        inside,
        cells,
        *edges,
        flat,
    )


def convolved(stack, kernel):
    return lax.conv_general_dilated(
        stack,
        kernel,
        (1, 1),
        "VALID",
        dimension_numbers=lax.ConvDimensionNumbers((2, 3, 0, 1), (3, 2, 0, 1), (2, 3, 0, 1)),
        preferred_element_type=jnp.float32,
    )


def packed(buf, out_ref, half):
    devices = out_ref.shape[0]

    def block(s, _):
        low = pl.multiple_of(s * half, half)
        left = buf[pl.ds(low, half), :]
        right = buf[pl.ds(devices * half + low, half), :]
        out_ref[s, pl.ds(0, half), :] = jnp.concatenate([left, right], axis=1).astype(jnp.bfloat16)

    lax.fori_loop(0, devices, block, None)


def unpacked(in_ref, buf, half):
    devices, _, lanes = in_ref.shape

    def block(s, _):
        low = pl.multiple_of(s * half, half)
        both = in_ref[s, pl.ds(0, half), :].astype(jnp.float32)
        buf[pl.ds(low, half), :] = both[:, : lanes // 2]
        buf[pl.ds(devices * half + low, half), :] = both[:, lanes // 2 :]

    lax.fori_loop(0, devices, block, None)


def each_arrival(devices, slots, count_ref, visit):
    half = slots // 2
    rows = devices * half

    def source(s, _):
        here = count_ref[s]
        for h in range(2):
            some = jnp.clip(here - h * half, 0, half)

            def group(j, _):
                for u in range(GROUP):
                    r = j * GROUP + u
                    visit(u, s * slots + h * half + r, h * rows + s * half + r)

            lax.fori_loop(0, (some + GROUP - 1) // GROUP, group, None)

    lax.fori_loop(0, devices, source, None)


def place_kernel(half, place_ref, vox_ref, rows_ref, out_ref, vox_out_ref, buf):
    def group(j, _):
        for u in range(GROUP):
            p = j * GROUP + u
            d = place_ref[p]
            buf[pl.ds(d, 1), :] = rows_ref[pl.ds(p, 1), :]
            vox_out_ref[d] = vox_ref[p]

    lax.fori_loop(0, rows_ref.shape[0] // GROUP, group, None)
    packed(buf, out_ref, half)


def splat_kernel(devices, slots, vox_ref, count_ref, got_ref, grid_ref, buf, *sums):
    unpacked(got_ref, buf, slots // 2)
    voxels, chans = grid_ref.shape

    def clear(t, _):
        for each in sums:
            each[pl.ds(pl.multiple_of(t * TILE, TILE), TILE), :] = jnp.zeros((TILE, chans), jnp.float32)

    lax.fori_loop(0, voxels // TILE, clear, None)

    def visit(u, k, r):
        v = vox_ref[k]
        each = sums[u % len(sums)]
        each[pl.ds(v, 1), :] += buf[pl.ds(r, 1), :]

    each_arrival(devices, slots, count_ref, visit)

    def finish(t, _):
        at = pl.ds(pl.multiple_of(t * TILE, TILE), TILE)
        total = sums[0][at, :]
        for each in sums[1:]:
            total += each[at, :]
        grid_ref[at, :] = total.astype(jnp.bfloat16)

    lax.fori_loop(0, voxels // TILE, finish, None)


def pick_kernel(devices, slots, vox_ref, count_ref, table_ref, out_ref, buf):
    def visit(u, k, r):
        buf[pl.ds(r, 1), :] = table_ref[pl.ds(vox_ref[k], 1), :]

    each_arrival(devices, slots, count_ref, visit)
    packed(buf, out_ref, slots // 2)


def collect_kernel(half, place_ref, back_ref, out_ref, buf):
    unpacked(back_ref, buf, half)

    def group(j, _):
        for u in range(GROUP):
            p = j * GROUP + u
            out_ref[pl.ds(p, 1), :] = buf[pl.ds(place_ref[p], 1), :]

    lax.fori_loop(0, out_ref.shape[0] // GROUP, group, None)


def call(kernel, out_shape, kinds, out_kinds, scratch, cost, *operands):
    where = {"s": pltpu.SMEM, "v": pltpu.VMEM, "a": pl.ANY}
    specs = [pl.BlockSpec(memory_space=where[k]) for k in out_kinds]
    return pl.pallas_call(
        kernel,
        out_shape=out_shape,
        in_specs=[pl.BlockSpec(memory_space=where[k]) for k in kinds],
        out_specs=specs if len(specs) > 1 else specs[0],
        scratch_shapes=scratch,
        compiler_params=pltpu.CompilerParams(vmem_limit_bytes=50 << 20),
        cost_estimate=pl.CostEstimate(flops=0, bytes_accessed=cost, transcendentals=0),
    )(*operands)


def ranks(owner, devices):
    span = 128
    chunks = owner.shape[0] // span
    marks = owner.reshape(chunks, span)[:, :, None] == jnp.arange(devices, dtype=jnp.int32)
    ones = marks.astype(jnp.bfloat16)
    before = (jnp.arange(span)[:, None] > jnp.arange(span)[None, :]).astype(jnp.bfloat16)
    inner = jnp.einsum("ij,cjo->cio", before, ones, preferred_element_type=jnp.float32)
    tallies = jnp.sum(ones.astype(jnp.float32), axis=1)
    ahead = (jnp.arange(chunks)[:, None] > jnp.arange(chunks)[None, :]).astype(jnp.bfloat16)
    starts = jnp.einsum("ij,jo->io", ahead, tallies.astype(jnp.bfloat16), preferred_element_type=jnp.float32)
    slot = jnp.sum(jnp.where(marks, inner + starts[:, None, :], 0.0), axis=2)
    return slot.reshape(-1).astype(jnp.int32), jnp.sum(tallies, axis=0).astype(jnp.int32)


def exchanged(x):
    return lax.all_to_all(x, AXES, split_axis=0, concat_axis=0, tiled=True)


def shards(point_feats, point_owner, point_voxel, weight, cotangent):
    n_narrow = lax.axis_size("narrow")
    n_region = lax.axis_size("region")
    devices = n_narrow * n_region
    chans, points_here = point_feats.shape
    slots = 2 * points_here // devices
    half = slots // 2
    rows = devices * half
    rows_x = cotangent.shape[1]
    voxels = rows_x * CY * NZ
    f32, bf16, i32 = jnp.float32, jnp.bfloat16, jnp.int32
    buffer = pltpu.VMEM((2 * rows, chans), f32)
    pairs = jax.ShapeDtypeStruct((devices, half, 2 * chans), bf16)
    spare = 16
    block = jax.ShapeDtypeStruct((devices, half + spare, 2 * chans), bf16)

    grads = cotangent.reshape(chans, rows_x, CY, NZ).transpose(1, 2, 3, 0)
    grad_edges = halos(grads, n_narrow, n_region, 0)
    point_feats, *grad_edges = lax.optimization_barrier((point_feats, *grad_edges))

    owner = point_owner[:, 0]
    slot, sent = ranks(owner, devices)
    place = (slot // half) * rows + owner * half + slot % half
    send, send_vox = call(
        functools.partial(place_kernel, half),
        (block, jax.ShapeDtypeStruct((2 * rows,), i32)),
        "ssv",
        "vs",
        [buffer],
        40 << 20,
        place,
        point_voxel,
        point_feats.T.astype(f32),
    )
    send_vox = send_vox.reshape(2, devices, half).transpose(1, 0, 2).reshape(devices, slots)
    filled = jnp.arange(slots, dtype=i32)[None, :] < sent[:, None]
    send_vox = jnp.where(filled, send_vox, voxels)
    digits = jnp.concatenate([send_vox // 128, send_vox % 128], axis=1).astype(bf16)
    digits = jnp.pad(digits, ((0, 0), (0, spare * 2 * chans - 2 * slots)))
    digits = digits.reshape(devices, spare, 2 * chans)
    got = exchanged(lax.dynamic_update_slice(send, digits, (0, half, 0)))
    digits = got[:, half:].reshape(devices, spare * 2 * chans).astype(i32)
    got_vox = digits[:, :slots] * 128 + digits[:, slots : 2 * slots]
    count = jnp.sum((got_vox < voxels).astype(i32), axis=1)
    add_at = got_vox.reshape(-1)
    pick_at = jnp.where(got_vox < voxels, got_vox, 0).reshape(-1)

    w = weight.reshape(3, 3, chans, 3, chans)
    backward = w[::-1, ::-1, :, ::-1, :].transpose(0, 1, 3, 2, 4).reshape(3, 3, 3 * chans, chans)
    forward = weight.reshape(3, 3, chans, 3 * chans).transpose(0, 1, 3, 2)

    grad_stack = stacked_depth(grads, grad_edges, n_narrow, n_region)
    table = convolved(grad_stack, backward).reshape(voxels, chans)
    picked = call(
        functools.partial(pick_kernel, devices, slots),
        pairs,
        "ssv",
        "v",
        [buffer],
        40 << 20,
        pick_at,
        count,
        table,
    )
    picked, got = lax.optimization_barrier((picked, got))
    back = exchanged(picked)

    grid = call(
        functools.partial(splat_kernel, devices, slots),
        jax.ShapeDtypeStruct((voxels, chans), bf16),
        "ssv",
        "v",
        [buffer] + [pltpu.VMEM((voxels + 8, chans), f32)] * 4,
        80 << 20,
        add_at,
        count,
        got,
    )
    cells = grid.reshape(rows_x, CY, NZ, chans)
    cell_edges = halos(cells, n_narrow, n_region, 1)
    flat = cotangent.reshape(chans, voxels)
    stack, kernels = stacked_depth(cells, cell_edges, n_narrow, n_region, flat)
    total_cells = rows_x * n_region * CY * n_narrow * NZ
    kernels, back = lax.optimization_barrier((kernels, back))
    parts = exchanged(kernels.reshape(devices, -1))
    mine = jnp.sum(parts, axis=0) * (1.0 / math.sqrt(total_cells))
    back, mine = lax.optimization_barrier((back, mine))
    everywhere = exchanged(jnp.broadcast_to(mine, (devices, mine.shape[0])))
    weight_grad = everywhere.reshape(9, chans, 3 * chans)

    result = convolved(stack, forward).astype(bf16)
    conv_out = result.transpose(3, 0, 1, 2).reshape(chans, rows_x, CY * NZ)

    point_rows = call(
        functools.partial(collect_kernel, half),
        jax.ShapeDtypeStruct((points_here, chans), f32),
        "sv",
        "v",
        [buffer],
        40 << 20,
        place,
        back,
    )
    return (conv_out, point_rows.T.astype(bf16), weight_grad)


def solution(mesh):
    in_specs = (
        P(None, AXES),
        P(AXES, None),
        P(AXES),
        P(),
        P(None, "region", "narrow"),
    )
    out_specs = (P(None, "region", "narrow"), P(None, AXES), P())
    return jax.shard_map(shards, mesh=mesh, in_specs=in_specs, out_specs=out_specs, check_vma=False)
```

```python
import functools
import math

import jax
import jax.numpy as jnp
from jax import lax
from jax.experimental import pallas as pl
from jax.experimental.pallas import tpu as pltpu
from jax.sharding import PartitionSpec as P

NZ = 64
CY = 8
AXES = ("narrow", "region")
GROUP = 8
TILE = 512


def halo_kernel(n_narrow, n_region, faces, ends, left, right, top, bottom, send, recv):
    n, r = lax.axis_index("narrow"), lax.axis_index("region")
    west, east = lax.rem(n + n_narrow - 1, n_narrow), lax.rem(n + 1, n_narrow)
    north, south = lax.rem(r + n_region - 1, n_region), lax.rem(r + 1, n_region)
    moves = [
        ((west, r), faces.at[0], right),
        ((east, r), faces.at[1], left),
        ((n, north), ends.at[0], bottom.at[pl.ds(1, CY)]),
        ((n, south), ends.at[1], top.at[pl.ds(1, CY)]),
        ((west, north), ends.at[0, 0], bottom.at[CY + 1]),
        ((east, north), ends.at[0, CY - 1], bottom.at[0]),
        ((west, south), ends.at[1, 0], top.at[CY + 1]),
        ((east, south), ends.at[1, CY - 1], top.at[0]),
    ]
    barrier = pltpu.get_barrier_semaphore()
    for device, _, _ in moves:
        pl.semaphore_signal(barrier, inc=1, device_id=device, device_id_type=pl.DeviceIdType.MESH)
    pl.semaphore_wait(barrier, len(moves))
    copies = [
        pltpu.make_async_remote_copy(
            src_ref=source,
            dst_ref=target,
            send_sem=send.at[i],
            recv_sem=recv.at[i],
            device_id=device,
            device_id_type=pl.DeviceIdType.MESH,
        )
        for i, (device, source, target) in enumerate(moves)
    ]
    for copy in copies:
        copy.start()
    for copy in copies:
        copy.wait()


def halos(grid, n_narrow, n_region, collective_id):
    rows_x, _, depth, chans = grid.shape
    half = depth // 2

    def paired(cells):
        return jnp.concatenate([cells[..., :half, :], cells[..., half:, :]], axis=-1)

    faces = paired(jnp.stack([grid[:, 0], grid[:, CY - 1]]))
    ends = paired(jnp.stack([grid[0], grid[rows_x - 1]]))
    side = jax.ShapeDtypeStruct((rows_x, half, 2 * chans), grid.dtype)
    end = jax.ShapeDtypeStruct((CY + 2, half, 2 * chans), grid.dtype)
    anywhere = pl.BlockSpec(memory_space=pl.ANY)
    return pl.pallas_call(
        functools.partial(halo_kernel, n_narrow, n_region),
        out_shape=(side, side, end, end),
        in_specs=[anywhere] * 2,
        out_specs=[anywhere] * 4,
        scratch_shapes=[pltpu.SemaphoreType.DMA((8,)), pltpu.SemaphoreType.DMA((8,))],
        compiler_params=pltpu.CompilerParams(collective_id=collective_id, has_side_effects=True),
        cost_estimate=pl.CostEstimate(flops=0, bytes_accessed=10 << 20, transcendentals=0),
    )(faces, ends)


def stack_kernel(inside_ref, center, *refs):
    far, (out, left, right, top, bottom, arrived) = refs[:4], refs[-6:]
    copies = [
        pltpu.make_async_copy(source, target, arrived.at[i])
        for i, (source, target) in enumerate(zip(far, (left, right, top, bottom)))
    ]
    for copy in copies:
        copy.start()
    rows_x, _, depth, chans = center.shape
    f32 = jnp.float32
    row = lax.broadcasted_iota(jnp.int32, (depth, chans), 0)
    west, east, north, south = [inside_ref[i] for i in range(4)]

    def spread(tile, keep=None):
        t = tile.astype(f32)
        if keep is not None:
            t = jnp.concatenate([t[:, :chans], t[:, chans:]], axis=0)
            t = jnp.where(keep > 0, t, 0.0)
        up = jnp.where(row == 0, 0.0, pltpu.roll(t, 1, 0))
        down = jnp.where(row == depth - 1, 0.0, pltpu.roll(t, depth - 1, 0))
        return jnp.concatenate([up, t, down], axis=1).astype(jnp.bfloat16)

    def plane(x, _):
        for y in range(CY):
            out[x + 1, y + 1] = spread(center[x, y])

    def sides(x, _):
        out[x + 1, 0] = spread(left[x], west)
        out[x + 1, CY + 1] = spread(right[x], east)

    lax.fori_loop(0, rows_x, plane, None)
    for copy in copies:
        copy.wait()
    lax.fori_loop(0, rows_x, sides, None)
    for at, end, keep in ((0, top, north), (rows_x + 1, bottom, south)):
        out[at, 0] = spread(end[0], keep * west)
        out[at, CY + 1] = spread(end[CY + 1], keep * east)
        for y in range(1, CY + 1):
            out[at, y] = spread(end[y], keep)


def stack_weight_kernel(inside_ref, center, left, right, top, bottom, flat, out, sums, *scratch):
    stack_kernel(inside_ref, center, left, right, top, bottom, out, *scratch)
    sums[...] = jnp.zeros_like(sums)
    plane_cells = CY * NZ

    def plane(x, _):
        here = flat[:, pl.ds(pl.multiple_of(x * plane_cells, plane_cells), plane_cells)]
        for a in range(3):
            for b in range(3):
                window = out[x + a, b : b + CY].reshape(plane_cells, out.shape[3])
                sums[3 * a + b] += jnp.dot(here, window, preferred_element_type=jnp.float32)

    lax.fori_loop(0, center.shape[0], plane, None)


def stacked_depth(cells, edges, n_narrow, n_region, flat=None):
    rows_x, _, depth, chans = cells.shape
    n, r = lax.axis_index("narrow"), lax.axis_index("region")
    inside = jnp.stack([n > 0, n < n_narrow - 1, r > 0, r < n_region - 1]).astype(jnp.int32)
    stack = jax.ShapeDtypeStruct((rows_x + 2, CY + 2, depth, 3 * chans), cells.dtype)
    scratch = [pltpu.VMEM(e.shape, e.dtype) for e in edges] + [pltpu.SemaphoreType.DMA((4,))]
    if flat is None:
        return call(stack_kernel, stack, "svaaaa", "v", scratch, 40 << 20, inside, cells, *edges)
    sums = jax.ShapeDtypeStruct((9, chans, 3 * chans), jnp.float32)
    return call(
        stack_weight_kernel,
        (stack, sums),
        "svaaaav",
        "vv",
        scratch,
        80 << 20,
        inside,
        cells,
        *edges,
        flat,
    )


def convolved(stack, kernel):
    return lax.conv_general_dilated(
        stack,
        kernel,
        (1, 1),
        "VALID",
        dimension_numbers=lax.ConvDimensionNumbers((2, 3, 0, 1), (3, 2, 0, 1), (2, 3, 0, 1)),
        preferred_element_type=jnp.float32,
    )


def packed(buf, out_ref, half):
    devices = out_ref.shape[0]

    def block(s, _):
        low = pl.multiple_of(s * half, half)
        left = buf[pl.ds(low, half), :]
        right = buf[pl.ds(devices * half + low, half), :]
        out_ref[s, pl.ds(0, half), :] = jnp.concatenate([left, right], axis=1).astype(jnp.bfloat16)

    lax.fori_loop(0, devices, block, None)


def unpacked(in_ref, buf, half):
    devices, _, lanes = in_ref.shape

    def block(s, _):
        low = pl.multiple_of(s * half, half)
        both = in_ref[s, pl.ds(0, half), :].astype(jnp.float32)
        buf[pl.ds(low, half), :] = both[:, : lanes // 2]
        buf[pl.ds(devices * half + low, half), :] = both[:, lanes // 2 :]

    lax.fori_loop(0, devices, block, None)


def each_arrival(devices, slots, count_ref, visit):
    half = slots // 2
    rows = devices * half

    def source(s, _):
        here = count_ref[s]
        for h in range(2):
            some = jnp.clip(here - h * half, 0, half)

            def group(j, _):
                for u in range(GROUP):
                    r = j * GROUP + u
                    visit(u, s * slots + h * half + r, h * rows + s * half + r)

            lax.fori_loop(0, (some + GROUP - 1) // GROUP, group, None)

    lax.fori_loop(0, devices, source, None)


def place_kernel(half, place_ref, vox_ref, rows_ref, out_ref, vox_out_ref, buf):
    def group(j, _):
        for u in range(GROUP):
            p = j * GROUP + u
            d = place_ref[p]
            buf[pl.ds(d, 1), :] = rows_ref[pl.ds(p, 1), :]
            vox_out_ref[d] = vox_ref[p]

    lax.fori_loop(0, rows_ref.shape[0] // GROUP, group, None)
    packed(buf, out_ref, half)


def splat_kernel(devices, slots, vox_ref, count_ref, got_ref, grid_ref, buf, *sums):
    unpacked(got_ref, buf, slots // 2)
    voxels, chans = grid_ref.shape

    def clear(t, _):
        for each in sums:
            each[pl.ds(pl.multiple_of(t * TILE, TILE), TILE), :] = jnp.zeros((TILE, chans), jnp.float32)

    lax.fori_loop(0, voxels // TILE, clear, None)

    def visit(u, k, r):
        v = vox_ref[k]
        each = sums[u % len(sums)]
        each[pl.ds(v, 1), :] += buf[pl.ds(r, 1), :]

    each_arrival(devices, slots, count_ref, visit)

    def finish(t, _):
        at = pl.ds(pl.multiple_of(t * TILE, TILE), TILE)
        total = sums[0][at, :]
        for each in sums[1:]:
            total += each[at, :]
        grid_ref[at, :] = total.astype(jnp.bfloat16)

    lax.fori_loop(0, voxels // TILE, finish, None)


def pick_kernel(devices, slots, vox_ref, count_ref, table_ref, out_ref, buf):
    def visit(u, k, r):
        buf[pl.ds(r, 1), :] = table_ref[pl.ds(vox_ref[k], 1), :]

    each_arrival(devices, slots, count_ref, visit)
    packed(buf, out_ref, slots // 2)


def collect_kernel(half, place_ref, back_ref, out_ref, buf):
    unpacked(back_ref, buf, half)

    def group(j, _):
        for u in range(GROUP):
            p = j * GROUP + u
            out_ref[pl.ds(p, 1), :] = buf[pl.ds(place_ref[p], 1), :]

    lax.fori_loop(0, out_ref.shape[0] // GROUP, group, None)


def call(kernel, out_shape, kinds, out_kinds, scratch, cost, *operands):
    where = {"s": pltpu.SMEM, "v": pltpu.VMEM, "a": pl.ANY}
    specs = [pl.BlockSpec(memory_space=where[k]) for k in out_kinds]
    return pl.pallas_call(
        kernel,
        out_shape=out_shape,
        in_specs=[pl.BlockSpec(memory_space=where[k]) for k in kinds],
        out_specs=specs if len(specs) > 1 else specs[0],
        scratch_shapes=scratch,
        compiler_params=pltpu.CompilerParams(vmem_limit_bytes=50 << 20),
        cost_estimate=pl.CostEstimate(flops=0, bytes_accessed=cost, transcendentals=0),
    )(*operands)


def ranks(owner, devices):
    span = 128
    chunks = owner.shape[0] // span
    marks = owner.reshape(chunks, span)[:, :, None] == jnp.arange(devices, dtype=jnp.int32)
    ones = marks.astype(jnp.bfloat16)
    before = (jnp.arange(span)[:, None] > jnp.arange(span)[None, :]).astype(jnp.bfloat16)
    inner = jnp.einsum("ij,cjo->cio", before, ones, preferred_element_type=jnp.float32)
    tallies = jnp.sum(ones.astype(jnp.float32), axis=1)
    ahead = (jnp.arange(chunks)[:, None] > jnp.arange(chunks)[None, :]).astype(jnp.bfloat16)
    starts = jnp.einsum("ij,jo->io", ahead, tallies.astype(jnp.bfloat16), preferred_element_type=jnp.float32)
    slot = jnp.sum(jnp.where(marks, inner + starts[:, None, :], 0.0), axis=2)
    return slot.reshape(-1).astype(jnp.int32), jnp.sum(tallies, axis=0).astype(jnp.int32)


def exchanged(x):
    return lax.all_to_all(x, AXES, split_axis=0, concat_axis=0, tiled=True)


def shards(point_feats, point_owner, point_voxel, weight, cotangent):
    n_narrow = lax.axis_size("narrow")
    n_region = lax.axis_size("region")
    devices = n_narrow * n_region
    chans, points_here = point_feats.shape
    slots = 2 * points_here // devices
    half = slots // 2
    rows = devices * half
    rows_x = cotangent.shape[1]
    voxels = rows_x * CY * NZ
    f32, bf16, i32 = jnp.float32, jnp.bfloat16, jnp.int32
    buffer = pltpu.VMEM((2 * rows, chans), f32)
    pairs = jax.ShapeDtypeStruct((devices, half, 2 * chans), bf16)
    spare = 16
    block = jax.ShapeDtypeStruct((devices, half + spare, 2 * chans), bf16)

    grads = cotangent.reshape(chans, rows_x, CY, NZ).transpose(1, 2, 3, 0)
    grad_edges = halos(grads, n_narrow, n_region, 0)
    point_feats, *grad_edges = lax.optimization_barrier((point_feats, *grad_edges))

    owner = point_owner[:, 0]
    slot, sent = ranks(owner, devices)
    place = (slot // half) * rows + owner * half + slot % half
    send, send_vox = call(
        functools.partial(place_kernel, half),
        (block, jax.ShapeDtypeStruct((2 * rows,), i32)),
        "ssv",
        "vs",
        [buffer],
        40 << 20,
        place,
        point_voxel,
        point_feats.T.astype(f32),
    )
    send_vox = send_vox.reshape(2, devices, half).transpose(1, 0, 2).reshape(devices, slots)
    filled = jnp.arange(slots, dtype=i32)[None, :] < sent[:, None]
    send_vox = jnp.where(filled, send_vox, voxels)
    digits = jnp.concatenate([send_vox // 128, send_vox % 128], axis=1).astype(bf16)
    digits = jnp.pad(digits, ((0, 0), (0, spare * 2 * chans - 2 * slots)))
    digits = digits.reshape(devices, spare, 2 * chans)
    got = exchanged(lax.dynamic_update_slice(send, digits, (0, half, 0)))
    digits = got[:, half:].reshape(devices, spare * 2 * chans).astype(i32)
    got_vox = digits[:, :slots] * 128 + digits[:, slots : 2 * slots]
    count = jnp.sum((got_vox < voxels).astype(i32), axis=1)
    add_at = got_vox.reshape(-1)
    pick_at = jnp.where(got_vox < voxels, got_vox, 0).reshape(-1)

    w = weight.reshape(3, 3, chans, 3, chans)
    backward = w[::-1, ::-1, :, ::-1, :].transpose(0, 1, 3, 2, 4).reshape(3, 3, 3 * chans, chans)
    forward = weight.reshape(3, 3, chans, 3 * chans).transpose(0, 1, 3, 2)

    grad_stack = stacked_depth(grads, grad_edges, n_narrow, n_region)
    table = convolved(grad_stack, backward).reshape(voxels, chans)
    picked = call(
        functools.partial(pick_kernel, devices, slots),
        pairs,
        "ssv",
        "v",
        [buffer],
        40 << 20,
        pick_at,
        count,
        table,
    )
    picked, got = lax.optimization_barrier((picked, got))
    back = exchanged(picked)

    grid = call(
        functools.partial(splat_kernel, devices, slots),
        jax.ShapeDtypeStruct((voxels, chans), bf16),
        "ssv",
        "v",
        [buffer] + [pltpu.VMEM((voxels + 8, chans), f32)] * 4,
        80 << 20,
        add_at,
        count,
        got,
    )
    cells = grid.reshape(rows_x, CY, NZ, chans)
    cell_edges = halos(cells, n_narrow, n_region, 1)
    flat = cotangent.reshape(chans, voxels)
    stack, kernels = stacked_depth(cells, cell_edges, n_narrow, n_region, flat)
    total_cells = rows_x * n_region * CY * n_narrow * NZ
    kernels, back = lax.optimization_barrier((kernels, back))
    parts = exchanged(kernels.reshape(devices, -1))
    mine = jnp.sum(parts, axis=0) * (1.0 / math.sqrt(total_cells))
    back, mine = lax.optimization_barrier((back, mine))
    everywhere = exchanged(jnp.broadcast_to(mine, (devices, mine.shape[0])))
    weight_grad = everywhere.reshape(9, chans, 3 * chans)

    result = convolved(stack, forward).astype(bf16)
    conv_out = result.transpose(3, 0, 1, 2).reshape(chans, rows_x, CY * NZ)

    point_rows = call(
        functools.partial(collect_kernel, half),
        jax.ShapeDtypeStruct((points_here, chans), f32),
        "sv",
        "v",
        [buffer],
        1 << 20,
        place,
        back,
    )
    return (conv_out, point_rows.T.astype(bf16), weight_grad)


def solution(mesh):
    in_specs = (
        P(None, AXES),
        P(AXES, None),
        P(AXES),
        P(),
        P(None, "region", "narrow"),
    )
    out_specs = (P(None, "region", "narrow"), P(None, AXES), P())
    return jax.shard_map(shards, mesh=mesh, in_specs=in_specs, out_specs=out_specs, check_vma=False)
```
